32 devices in a mesh: exp: 16 (over z, y, core), ctx: 2 (over x).
Axes of the slice: x: 2, y: 2, z: 4, core: 2. Of those that a mesh axis runs over, the one named last changes fastest.
Arguments:
- inputs: bfloat16 [4096, 1024], P(('exp', 'ctx')), may hold values from -30 to 30
- selected: int32 [32, 32], P(None, 'ctx'), may hold values from 0 to 4095, as said below
- selection_gate: float32 [32, 32], P('exp', 'ctx'), may hold values from 0.1 to 1
- gate_weight: bfloat16 [32, 1024, 2048], P('exp', None, 'ctx'), may hold values from -0.1875 to 0.1875
- up_weight: bfloat16 [32, 1024, 2048], P('exp', None, 'ctx'), may hold values from -0.1875 to 0.1875
- down_weight: bfloat16 [32, 2048, 1024], P('exp', 'ctx'), may hold values from -0.125 to 0.125
- norm_gain: float32 [1024], replicated, may hold values from 0.5 to 1.5
- query_weight: bfloat16 [1024, 1024], P('exp'), may hold values from -1 to 1
- key_weight: bfloat16 [1024, 1024], P('exp'), may hold values from -1 to 1
- value_weight: bfloat16 [1024, 1024], P('exp'), may hold values from -0.1875 to 0.1875
- train_count: int32 [16], P('exp'), may hold values from 64 to 255
Outputs:
- layer_out: bfloat16 [4096, 1024], P(('exp', 'ctx'))
- context: bfloat16 [4096, 1024], P(('exp', 'ctx'))
The draws below stay inside these ranges and needn't reach their ends.
Inputs may be any that keep to these rules, and one draw needn't show every extreme that they name: `selected`: each expert's 32 entries are distinct rows. Entries c * 16 to (c + 1) * 16 - 1 of every expert name rows at positions c * 128 to (c + 1) * 128 - 1 of their tables. At most 2 entries of one expert name rows of one block of 128 rows, and in each group of 16 entries of each expert some block gives exactly 2.
All inputs are finite; a program needn't handle non-finite values.
Results may differ from the reference program's by a relative error of at most 0.017.
Values may be sent and summed in bfloat16 or wider, within the bound.
A program may use at most 64 MiB of HBM per device.

```python
import jax
import jax.numpy as jnp
from jax import lax

D = 1024
FF = 2048
HEADS = 16
HEAD_DIM = 64
R_DEV = 128
GROUP_TAKE = 16
TABLES = 16
TABLE = 256
ROWS = 4096
EXPERTS = 32
CAP = 32
MOST = 2
N_EXP = 16
N_CTX = 2


def log_even(key, grid_shape, low_end, high_end):
    return jnp.exp(jax.random.uniform(key, grid_shape, jnp.float32, jnp.log(low_end), jnp.log(high_end)))


def draw_inputs(key, part):
    key_list = jax.random.split(jax.random.fold_in(key, 21), 3)
    row_scale = log_even(key_list[0], (ROWS, 1), 0.3, 3.0)
    col_scale = log_even(key_list[1], (1, D), 0.3, 3.0)
    noise_part = jax.random.normal(key_list[2], (ROWS, D), jnp.float32)
    values = row_scale * col_scale * noise_part
    return jnp.clip(values, -30.0, 30.0).astype(jnp.bfloat16)


def drawn_weight(key, salt):
    base_matrix = jax.random.normal(jax.random.fold_in(key, salt), (D, D), jnp.float32) * D ** (-0.5)
    return jnp.clip(base_matrix, -1.0, 1.0).astype(jnp.bfloat16)


def draw_query_weight(key, part):
    return drawn_weight(key, 51)


def draw_key_weight(key, part):
    return drawn_weight(key, 52)


def draw_selected(key, part):
    key_list = jax.random.split(jax.random.fold_in(key, 41), 7)
    token_total = N_EXP * MOST
    grid_shape = (EXPERTS, N_CTX)
    hot_table = jnp.minimum(jax.random.randint(key_list[0], grid_shape, 0, N_EXP), jax.random.randint(key_list[1], grid_shape, 0, N_EXP))
    busy_level = jax.random.randint(key_list[2], (N_EXP,), 0, 4)
    token_index = jnp.arange(token_total, dtype=jnp.int32)
    token_table = token_index // MOST
    token_copy = token_index % MOST
    noise_part = jax.random.randint(key_list[3], grid_shape + (token_total,), 0, 65536)
    score_int = jnp.where(token_table[None, None, :] == hot_table[:, :, None], 1 << 30, 0) + jnp.take(busy_level, token_table)[None, None, :] * (1 << 28) + noise_part * 4096 + token_index[None, None, :]
    chosen = lax.top_k(score_int, GROUP_TAKE)[1].astype(jnp.int32)
    table_id = chosen // MOST
    copy_id = jnp.take(token_copy, chosen)
    offset_all = jax.random.randint(key_list[4], grid_shape + (N_EXP,), 0, R_DEV)
    stride_all = jax.random.randint(key_list[5], grid_shape + (N_EXP,), 1, R_DEV // MOST + 1)
    offset_pick = jnp.take_along_axis(offset_all, table_id, axis=2)
    stride_pick = jnp.take_along_axis(stride_all, table_id, axis=2)
    local_row = (offset_pick + copy_id * stride_pick) % R_DEV
    group_id = jnp.arange(N_CTX, dtype=jnp.int32)[None, :, None]
    row_ids = (table_id * N_CTX + group_id) * R_DEV + local_row
    shuffle_key = jax.random.randint(key_list[6], grid_shape + (GROUP_TAKE,), 0, 65536) * 1024 + jnp.arange(GROUP_TAKE, dtype=jnp.int32)
    shuffle_order = lax.top_k(shuffle_key, GROUP_TAKE)[1]
    row_ids = jnp.take_along_axis(row_ids, shuffle_order, axis=2)
    return row_ids.reshape(EXPERTS, CAP).astype(jnp.int32)


def set_ends(drawn, own_key, smallest, high):
    spot = [jax.random.randint(jax.random.fold_in(own_key, axis), (), 0, length) for axis, length in enumerate(drawn.shape)]
    longest = drawn.shape.index(max(drawn.shape))
    neighbour = spot[:longest] + [(spot[longest] + 1) % drawn.shape[longest]] + spot[longest + 1:]
    return drawn.at[tuple(spot)].set(smallest).at[tuple(neighbour)].set(high)


def block_scale(key, dims, shards, smallest, top_value):
    level, own = 1.0, jax.random.fold_in(key, 6)
    for dim, parts in shards:
        steps = jnp.exp(jax.random.uniform(jax.random.fold_in(own, dim), (parts,), jnp.float32, smallest / len(shards), top_value / len(shards)))
        level = level * jnp.repeat(steps, dims[dim] // parts).reshape([-1 if axis == dim else 1 for axis in range(len(dims))])
    return level


def scatter_about(key, extent, scale, limit, pieces=(), kind=jnp.bfloat16):
    values = scale * jax.random.normal(key, extent, jnp.float32)
    if pieces:
        values = values * block_scale(key, extent, pieces, -0.22, 0.18)
    return jnp.clip(values, -limit, limit).astype(kind)


def setup_inputs(seed: int = 0) -> dict:
    key_of = jax.random.split(jax.random.key(seed), 12)
    return {
        "inputs": draw_inputs(jax.random.fold_in(key_of[11], 71), 0),
        "selected": draw_selected(jax.random.fold_in(key_of[11], 71), 0),
        "selection_gate": jnp.clip(0.1 + 0.9 * jax.random.uniform(key_of[2], (EXPERTS, CAP), jnp.float32) ** block_scale(key_of[2], (EXPERTS, CAP), ((0, 16), (1, 2)), -0.2, 0.2), 0.1, 1.0),
        "gate_weight": scatter_about(key_of[3], (EXPERTS, D, FF), D ** -0.5, 0.1875, ((0, 16), (2, 2))),
        "up_weight": scatter_about(key_of[4], (EXPERTS, D, FF), D ** -0.5, 0.1875, ((0, 16), (2, 2))),
        "down_weight": scatter_about(key_of[5], (EXPERTS, FF, D), FF ** -0.5, 0.125, ((0, 16), (1, 2))),
        "norm_gain": jnp.clip(1.0 + 0.1 * jax.random.normal(key_of[6], (D,), jnp.float32), 0.5, 1.5),
        "query_weight": draw_query_weight(jax.random.fold_in(key_of[11], 71), 0),
        "key_weight": draw_key_weight(jax.random.fold_in(key_of[11], 71), 0),
        "value_weight": scatter_about(key_of[9], (D, D), D ** -0.5, 0.1875, ((0, 16),)),
        "train_count": set_ends(jax.random.randint(key_of[10], (TABLES,), TABLE // 4, TABLE), jax.random.fold_in(key_of[10], 1), TABLE // 4, TABLE - 1).astype(jnp.int32),
    }


EPSILON = 1e-06
MASKED = -1e+30

def expert_terms(inputs, selected, selection_gate, gate_weight, up_weight, down_weight):

    def one_expert(operands):
        chosen_rows, gate_row, gate_matrix, up_matrix, down_matrix = operands
        chosen = jnp.take(inputs, chosen_rows, axis=0)
        gate_part = jnp.dot(chosen, gate_matrix, preferred_element_type=jnp.float32)
        up_part = jnp.dot(chosen, up_matrix, preferred_element_type=jnp.float32)
        hidden = (jax.nn.silu(gate_part) * up_part).astype(jnp.bfloat16)
        expert_out = jnp.dot(hidden, down_matrix, preferred_element_type=jnp.float32)
        return (gate_row[:, None] * expert_out).astype(jnp.bfloat16)
    return lax.map(one_expert, (selected, selection_gate, gate_weight, up_weight, down_weight))

def table_attention(operands, norm_gain, query_weight, key_weight, value_weight):
    table_rows, train_rows = operands
    widened = table_rows.astype(jnp.float32)
    scale_row = lax.rsqrt(lax.optimization_barrier(jnp.mean(widened * widened, axis=1, keepdims=True)) + EPSILON)
    normed = (widened * scale_row * norm_gain).astype(jnp.bfloat16)
    query_rows = jnp.dot(normed, query_weight, preferred_element_type=jnp.float32).astype(jnp.bfloat16)
    key_rows = jnp.dot(normed, key_weight, preferred_element_type=jnp.float32).astype(jnp.bfloat16)
    value_rows = jnp.dot(normed, value_weight, preferred_element_type=jnp.float32).astype(jnp.bfloat16)
    query_heads = query_rows.astype(jnp.float32).reshape(TABLE, HEADS, HEAD_DIM)
    key_heads = key_rows.astype(jnp.float32).reshape(TABLE, HEADS, HEAD_DIM)
    value_heads = value_rows.astype(jnp.float32).reshape(TABLE, HEADS, HEAD_DIM)
    scores = jnp.einsum('qhd,khd->hqk', query_heads, key_heads) * HEAD_DIM ** (-0.5)
    allowed = jnp.arange(TABLE, dtype=jnp.int32) < train_rows
    scores = jnp.where(allowed, scores, MASKED)
    top_score = lax.optimization_barrier(jnp.max(scores, axis=2, keepdims=True))
    raw_weights = jnp.where(allowed, jnp.exp(scores - top_score), 0.0)
    denominator = lax.optimization_barrier(jnp.sum(raw_weights, axis=2))
    rounded = lax.optimization_barrier(raw_weights.astype(jnp.bfloat16)).astype(jnp.float32)
    context = jnp.einsum('hqk,khd->hqd', rounded, value_heads) / denominator[:, :, None]
    return jnp.transpose(context, (1, 0, 2)).reshape(TABLE, D).astype(jnp.bfloat16)

def reference(inputs, selected, selection_gate, gate_weight, up_weight, down_weight, norm_gain, query_weight, key_weight, value_weight, train_count):
    weighted = expert_terms(inputs, selected, selection_gate, gate_weight, up_weight, down_weight)
    moe_sum = jax.ops.segment_sum(weighted.reshape(-1, D).astype(jnp.float32), selected.reshape(-1), num_segments=ROWS)
    layer_out = (inputs.astype(jnp.float32) + moe_sum).astype(jnp.bfloat16)

    def per_table(operands):
        return table_attention(operands, norm_gain, query_weight, key_weight, value_weight)
    context = lax.map(per_table, (layer_out.reshape(TABLES, TABLE, D), train_count))
    return (layer_out, context.reshape(ROWS, D))
```

```python
import functools

import jax
import jax.numpy as jnp
from jax import lax
from jax.experimental import pallas as pl
from jax.experimental.pallas import tpu as pltpu
from jax.sharding import PartitionSpec as P

HEAD_DIM = 64


EPSILON = 1e-06
MASKED = -1e30


def block_rank(block_ids):
    slot_count = block_ids.shape[1]
    earlier = jnp.arange(slot_count)[:, None] > jnp.arange(slot_count)[None, :]
    same_block = block_ids[:, :, None] == block_ids[:, None, :]
    return jnp.sum(jnp.where(same_block & earlier[None], 1, 0), axis=2).astype(jnp.int32)


def local(
    inputs,
    selected,
    selection_gate,
    gate_weight,
    up_weight,
    down_weight,
    norm_gain,
    query_weight,
    key_weight,
    value_weight,
    train_count,
):
    exp_count = lax.axis_size("exp")
    ctx_count = lax.axis_size("ctx")
    exp_index = lax.axis_index("exp")
    ctx_index = lax.axis_index("ctx")
    row_count, model_width = inputs.shape
    expert_local = gate_weight.shape[0]
    group_take = selected.shape[1]
    most_rows = max(2, (2 * group_take + exp_count - 1) // exp_count)
    block_ids = selected // row_count
    slot_rank = block_rank(block_ids)
    own_block = exp_index * ctx_count + ctx_index
    is_mine = block_ids == own_block
    local_row = selected - own_block * row_count
    rank_slots = jnp.arange(most_rows, dtype=jnp.int32)
    slot_hit = is_mine[:, None, :] & (slot_rank[:, None, :] == rank_slots[None, :, None])
    pick_row = jnp.sum(jnp.where(slot_hit, local_row[:, None, :], 0), axis=2)
    filled = jnp.any(slot_hit, axis=2).reshape(-1)
    picked = jnp.take(inputs, pick_row.reshape(-1), axis=0)
    outgoing = jnp.where(filled[:, None], picked, jnp.zeros_like(picked)).reshape(
        exp_count, -1, model_width
    )
    incoming = lax.all_to_all(outgoing, "exp", split_axis=0, concat_axis=0, tiled=True)
    my_blocks = lax.dynamic_slice_in_dim(block_ids, exp_index * expert_local, expert_local, 0)
    my_rank = lax.dynamic_slice_in_dim(slot_rank, exp_index * expert_local, expert_local, 0)
    my_source = my_blocks // ctx_count
    expert_slot = jnp.arange(expert_local, dtype=jnp.int32)[:, None]
    flat_index = (my_source * expert_local + expert_slot) * most_rows + my_rank
    compact = jnp.take(incoming.reshape(-1, model_width), flat_index.T.reshape(-1), axis=0)
    compact = compact.reshape(group_take, expert_local, model_width)
    block_rows = lax.all_gather(compact, "ctx", axis=0, tiled=True)
    gate_part = jnp.einsum(
        "nxd,xdf->nxf", block_rows, gate_weight, preferred_element_type=jnp.float32
    )
    up_part = jnp.einsum("nxd,xdf->nxf", block_rows, up_weight, preferred_element_type=jnp.float32)
    hidden = (jax.nn.silu(gate_part) * up_part).astype(jnp.bfloat16)
    summed = lax.psum_scatter(
        jnp.einsum("nxf,xfd->nxd", hidden, down_weight, preferred_element_type=jnp.float32).astype(
            jnp.bfloat16
        ),
        "ctx",
        scatter_dimension=0,
        tiled=True,
    ).astype(jnp.float32)
    weighted = (summed * selection_gate.T[:, :, None]).astype(jnp.bfloat16)
    source_ids = jnp.arange(exp_count, dtype=jnp.int32)
    expert_ids = jnp.arange(expert_local, dtype=jnp.int32)[None, :, None, None]
    slot_index = jnp.arange(group_take, dtype=jnp.int32)[None, None, None, :]
    reply_hit = (my_source[None, :, None, :] == source_ids[:, None, None, None]) & (
        my_rank[None, :, None, :] == rank_slots[None, None, :, None]
    )
    reply_pick = jnp.sum(jnp.where(reply_hit, slot_index * expert_local + expert_ids, 0), axis=3)
    reply_filled = jnp.any(reply_hit, axis=3).reshape(-1)
    reply_rows = jnp.take(weighted.reshape(-1, model_width), reply_pick.reshape(-1), axis=0)
    reply_rows = jnp.where(reply_filled[:, None], reply_rows, jnp.zeros_like(reply_rows)).reshape(
        exp_count, -1, model_width
    )
    returned = lax.all_to_all(reply_rows, "exp", split_axis=0, concat_axis=0, tiled=True)
    owner_hit = (
        pick_row.reshape(-1)[None, :] == jnp.arange(row_count, dtype=jnp.int32)[:, None]
    ) & filled[None, :]
    moe_sum = jnp.dot(
        owner_hit.astype(jnp.bfloat16),
        returned.reshape(-1, model_width),
        preferred_element_type=jnp.float32,
    )
    layer_out = (inputs.astype(jnp.float32) + moe_sum).astype(jnp.bfloat16)
    widened = layer_out.astype(jnp.float32)
    scale_row = lax.rsqrt(jnp.mean(widened * widened, axis=1, keepdims=True) + EPSILON)
    normed = (widened * scale_row * norm_gain).astype(jnp.bfloat16)
    score_scale = HEAD_DIM ** (-0.5)
    train_rows = train_count[0]
    head_cols = model_width // ctx_count
    col_start = ctx_index * head_cols
    query_cols = lax.dynamic_slice_in_dim(query_weight, col_start, head_cols, 1)
    key_cols = lax.dynamic_slice_in_dim(key_weight, col_start, head_cols, 1)
    value_cols = lax.dynamic_slice_in_dim(value_weight, col_start, head_cols, 1)
    gathered = (
        lax.all_gather(query_cols, "exp", axis=0, tiled=True),
        lax.all_gather(key_cols, "exp", axis=0, tiled=True),
        lax.all_gather(value_cols, "exp", axis=0, tiled=True),
    )
    joined = jnp.concatenate(gathered, axis=1)
    table_proj = jnp.dot(
        lax.all_gather(normed, "ctx", axis=0, tiled=True),
        joined,
        preferred_element_type=jnp.float32,
    ).astype(jnp.bfloat16)
    table_count = table_proj.shape[0]
    local_heads = head_cols // HEAD_DIM
    query_all = table_proj[:, :head_cols].reshape(table_count, local_heads, HEAD_DIM)
    key_all = table_proj[:, head_cols : 2 * head_cols].reshape(table_count, local_heads, HEAD_DIM)
    value_all = table_proj[:, 2 * head_cols :].reshape(table_count, local_heads, HEAD_DIM)
    block_size = min(table_count, 512)
    allowed = jnp.arange(table_count, dtype=jnp.int32) < train_rows

    def attend_block(query_block):
        scores = (
            jnp.einsum("qhd,khd->hqk", query_block, key_all, preferred_element_type=jnp.float32)
            * score_scale
        )
        scores = jnp.where(allowed, scores, MASKED)
        top_score = jnp.max(scores, axis=2, keepdims=True)
        weights = jnp.where(allowed, jnp.exp(scores - top_score), 0.0)
        denominator = jnp.sum(weights, axis=2)
        blended = jnp.einsum(
            "hqk,khd->qhd",
            weights.astype(jnp.bfloat16),
            value_all,
            preferred_element_type=jnp.float32,
        )
        return (blended / denominator.T[:, :, None]).astype(jnp.bfloat16)

    head_context = lax.map(
        attend_block,
        query_all.reshape(table_count // block_size, block_size, local_heads, HEAD_DIM),
    )
    context = lax.all_to_all(
        head_context.reshape(table_count, head_cols), "ctx", split_axis=0, concat_axis=1, tiled=True
    )
    return (layer_out, context)


MESH = pl.DeviceIdType.MESH
MOST = 2
FOLD = 4
NEVER = 1 << 20
VMEM_LIMIT = 60 * 1024 * 1024


def iota(shape, dim):
    return lax.broadcasted_iota(jnp.int32, shape, dim)


def onehot(condition):
    return jnp.where(condition, 1.0, 0.0).astype(jnp.bfloat16)


def dot(a, b):
    return jnp.dot(a, b, preferred_element_type=jnp.float32)


def dot_t(a, b, contract):
    return lax.dot_general(a, b, (contract, ((), ())), preferred_element_type=jnp.float32)


def fused(
    exp_count,
    ctx_count,
    x_ref,
    sel_ref,
    gate_ref,
    wg_hbm,
    wu_hbm,
    wd_hbm,
    gain_ref,
    q_hbm,
    k_hbm,
    v_hbm,
    count_ref,
    layer_ref,
    context_ref,
    wg,
    wu,
    wd,
    weights,
    out_rows,
    in_rows,
    reply_rows,
    back_rows,
    gates,
    table,
    proj,
    away,
    spread,
    hbm_sem,
    col_sem,
    go_send,
    go_recv,
    back_send,
    back_recv,
    gate_send,
    gate_recv,
    z_send,
    z_recv,
    y_send,
    y_recv,
    c_send,
    c_recv,
    row_send,
    row_recv,
    out_send,
    out_recv,
):
    e = lax.axis_index("exp")
    c = lax.axis_index("ctx")
    rows, width = x_ref.shape
    experts, take = sel_ref.shape
    local_experts = wg.shape[0]
    devices = exp_count * ctx_count
    me = e * ctx_count + c
    group = local_experts * MOST
    block = group * FOLD
    fold = width // FOLD
    shard = q_hbm.shape[0]
    head_cols = width // ctx_count
    padded = local_experts * devices * MOST

    barrier = pltpu.get_barrier_semaphore()

    def greet(d, carry):
        to = lax.rem(me + d, devices)
        pl.semaphore_signal(
            barrier, inc=1, device_id=(to // ctx_count, lax.rem(to, ctx_count)), device_id_type=MESH
        )
        return carry

    lax.fori_loop(1, devices, greet, 0)

    def rows_of(o):
        return weights.at[pl.ds(pl.multiple_of(o * shard, shard), shard), :]

    own_cols = []
    for n, ref in enumerate((q_hbm, k_hbm, v_hbm)):
        copy = pltpu.make_async_copy(
            ref.at[:, pl.ds(pl.multiple_of(c * head_cols, head_cols), head_cols)],
            weights.at[
                pl.ds(pl.multiple_of(e * shard, shard), shard), pl.ds(n * head_cols, head_cols)
            ],
            col_sem.at[n],
        )
        copy.start()
        own_cols.append(copy)
    loads = []
    for x in range(local_experts):
        for n, (hbm, vmem) in enumerate(((wg_hbm, wg), (wu_hbm, wu), (wd_hbm, wd))):
            copy = pltpu.make_async_copy(hbm.at[x], vmem.at[x], hbm_sem.at[x * 3 + n])
            copy.start()
            loads.append(copy)

    selected = sel_ref[...]
    start = me * rows
    mine = (selected >= start) & (selected < start + rows)
    offset = selected - start
    low = jnp.min(jnp.where(mine, offset, NEVER), axis=1, keepdims=True)
    high = jnp.max(jnp.where(mine, offset, -1), axis=1, keepdims=True)
    high = jnp.where(high == low, NEVER, high)
    lanes = iota((experts, rows), 1)
    picks = (onehot(lanes == low), onehot(lanes == high))

    def spread_picks(count, per_expert_device):
        m = iota((count, experts), 0)
        j = m // (block * per_expert_device)
        want = j * local_experts + lax.rem(m, group) // MOST
        hit = iota((count, experts), 1) == want
        rank = lax.rem(m, MOST)
        return dot(onehot(hit & (rank == 0)), picks[0]) + dot(onehot(hit & (rank == 1)), picks[1])

    out_count = exp_count * block
    everything = dot(spread_picks(out_count, 1).astype(jnp.bfloat16), x_ref[...])
    part = lax.rem(iota((out_count, 1), 0), block) // group
    folded = jnp.zeros((out_count, fold), jnp.float32)
    for f in range(FOLD):
        folded = jnp.where(part == f, everything[:, f * fold : (f + 1) * fold], folded)
    out_rows[...] = folded.astype(jnp.bfloat16)

    in_count = devices * block
    spread[...] = spread_picks(in_count, ctx_count).astype(jnp.bfloat16)

    pair = iota((devices * MOST, 1), 0)
    owner = pair // MOST
    rank = lax.rem(pair, MOST)
    for x in range(local_experts):
        sel_x = sel_ref[pl.ds(e * local_experts + x, 1), :]
        gate_x = gate_ref[pl.ds(x, 1), :]
        off = jnp.broadcast_to(sel_x, (devices * MOST, take)) - owner * rows
        own = (off >= 0) & (off < rows) & (lax.rem(owner, ctx_count) == c)
        lo = jnp.min(jnp.where(own, off, NEVER), axis=1, keepdims=True)
        hi = jnp.max(jnp.where(own, off, -1), axis=1, keepdims=True)
        want = jnp.where(rank == 0, lo, jnp.where(hi == lo, NEVER, hi))
        value = jnp.sum(
            jnp.where(own & (off == want), jnp.broadcast_to(gate_x, off.shape), 0.0),
            axis=1,
            keepdims=True,
        )
        gates[0, x * devices * MOST : (x + 1) * devices * MOST, :] = jnp.broadcast_to(
            value, (devices * MOST, gates.shape[2])
        )

    def slot(ref, index):
        return ref.at[pl.ds(pl.multiple_of(index * block, block), block), :]

    def go_copy(d):
        to = lax.rem(me + d, devices)
        return pltpu.make_async_remote_copy(
            src_ref=slot(out_rows, to // ctx_count),
            dst_ref=slot(in_rows, me),
            send_sem=go_send.at[d],
            recv_sem=go_recv.at[d],
            device_id=(to // ctx_count, lax.rem(to, ctx_count)),
            device_id_type=MESH,
        )

    def back_copy(d):
        to = lax.rem(me + d, devices)
        return pltpu.make_async_remote_copy(
            src_ref=slot(reply_rows, to),
            dst_ref=slot(back_rows, me),
            send_sem=back_send.at[d],
            recv_sem=back_recv.at[d],
            device_id=(to // ctx_count, lax.rem(to, ctx_count)),
            device_id_type=MESH,
        )

    def arrived(ref, sems, d):
        source = lax.rem(me + devices - d, devices)
        pltpu.make_async_remote_copy(
            src_ref=slot(ref, source),
            dst_ref=slot(ref, source),
            send_sem=sems.at[d],
            recv_sem=sems.at[d],
            device_id=(source // ctx_count, lax.rem(source, ctx_count)),
            device_id_type=MESH,
        ).wait_recv()

    def gate_copy(d):
        return pltpu.make_async_remote_copy(
            src_ref=gates.at[0],
            dst_ref=gates.at[d],
            send_sem=gate_send.at[d],
            recv_sem=gate_recv.at[d],
            device_id=(e, lax.rem(c + d, ctx_count)),
            device_id_type=MESH,
        )

    depth = exp_count // 4
    z, y, k = e // 4, lax.rem(e // 2, 2), lax.rem(e, 2)

    def member(z_at, y_at, k_at):
        return z_at * 4 + y_at * 2 + k_at

    def weight_copy(o, to, send, recv):
        return pltpu.make_async_remote_copy(
            src_ref=rows_of(o),
            dst_ref=rows_of(o),
            send_sem=send,
            recv_sem=recv,
            device_id=(to, c),
            device_id_type=MESH,
        )

    y_peer = member(z, 1 - y, k)
    k_peer = member(z, y, 1 - k)

    def z_copy(d):
        return weight_copy(e, member(lax.rem(z + d, depth), y, k), z_send.at[d], z_recv.at[d])

    def behind(d):
        return lax.rem(z + depth - d, depth)

    def y_copy(d):
        return weight_copy(member(behind(d), y, k), y_peer, y_send.at[d], y_recv.at[d])

    def y_in(d):
        return weight_copy(member(behind(d), 1 - y, k), y_peer, y_send.at[d], y_recv.at[d])

    def z_in(d):
        return weight_copy(member(behind(d), y, k), y_peer, z_send.at[d], z_recv.at[d])

    def k_copy(d, across):
        y_at = 1 - y if across else y
        n = d + depth * across
        return weight_copy(member(behind(d), y_at, k), k_peer, c_send.at[n], c_recv.at[n])

    def k_in(d, across):
        y_at = 1 - y if across else y
        n = d + depth * across
        return weight_copy(member(behind(d), y_at, 1 - k), k_peer, c_send.at[n], c_recv.at[n])

    def relay_z(d):
        z_in(d).wait_recv()
        y_copy(d).start()
        k_copy(d, 0).start()

    def relay_y(d):
        y_in(d).wait_recv()
        k_copy(d, 1).start()

    pl.semaphore_wait(barrier, devices - 1)

    def start_go(d, carry):
        go_copy(d).start()
        return carry

    lax.fori_loop(1, devices, start_go, 0)
    for d in range(1, ctx_count):
        gate_copy(d).start()
    for copy in own_cols:
        copy.wait()
    for d in range(1, depth):
        z_copy(d).start()
    y_copy(0).start()
    k_copy(0, 0).start()

    in_rows[pl.ds(pl.multiple_of(me * block, block), block), :] = out_rows[
        pl.ds(pl.multiple_of(e * block, block), block), :
    ]
    m = iota((padded, in_count), 1)
    n = iota((padded, in_count), 0)
    per = devices * MOST
    matches = (
        (m // block == lax.rem(n, per) // MOST)
        & (lax.rem(m, group) // MOST == n // per)
        & (lax.rem(m, MOST) == lax.rem(n, MOST))
    )
    unfold = [
        onehot(matches & (lax.rem(m, block) // group == f)) for f in range(FOLD)
    ]

    def wait_go(d, carry):
        arrived(in_rows, go_recv, d)
        return carry

    lax.fori_loop(1, devices, wait_go, 0)
    received = in_rows[...]
    tokens = jnp.concatenate(
        [dot(u, received).astype(jnp.bfloat16) for u in unfold], axis=1
    )
    for d in range(1, ctx_count):
        gate_copy(d).wait_recv()
    parts = []
    for x in range(local_experts):
        chosen = tokens[x * per : (x + 1) * per, :]
        loads[3 * x].wait()
        gate_part = dot(chosen, wg[x])
        loads[3 * x + 1].wait()
        up_part = dot(chosen, wu[x])
        hidden = (gate_part / (1.0 + jnp.exp(-gate_part)) * up_part).astype(jnp.bfloat16)
        loads[3 * x + 2].wait()
        expert_out = dot(hidden, wd[x])
        factor = gates[0, x * per : (x + 1) * per, 0:1]
        for d in range(1, ctx_count):
            factor = factor + gates[d, x * per : (x + 1) * per, 0:1]
        parts.append((expert_out * factor).astype(jnp.bfloat16))
        if x == 0:
            for d in range(1, min(2, depth)):
                relay_z(d)
            relay_y(0)
    weighted = jnp.concatenate(parts, axis=0)
    m = iota((in_count, padded), 0)
    n = iota((in_count, padded), 1)
    back = onehot(
        (m // block == lax.rem(n, per) // MOST)
        & (lax.rem(m, group) // MOST == n // per)
        & (lax.rem(m, MOST) == lax.rem(n, MOST))
    )
    part = lax.rem(iota((in_count, 1), 0), block) // group
    folded = jnp.zeros((in_count, fold), jnp.float32)
    for f in range(FOLD):
        folded = jnp.where(part == f, dot(back, weighted[:, f * fold : (f + 1) * fold]), folded)
    reply_rows[...] = folded.astype(jnp.bfloat16)

    def start_back(d, carry):
        back_copy(d).start()
        return carry

    lax.fori_loop(1, devices, start_back, 0)
    back_rows[pl.ds(pl.multiple_of(me * block, block), block), :] = reply_rows[
        pl.ds(pl.multiple_of(me * block, block), block), :
    ]
    for d in range(2, depth):
        relay_z(d)

    def wait_back(d, carry):
        arrived(back_rows, back_recv, d)
        return carry

    lax.fori_loop(1, devices, wait_back, 0)
    returned = back_rows[...]
    moe = []
    for f in range(FOLD):
        hits = jnp.where(part == f, spread[...], jnp.zeros_like(spread[...]))
        moe.append(dot_t(hits, returned, ((0,), (0,))))
    layer = (x_ref[...].astype(jnp.float32) + jnp.concatenate(moe, axis=1)).astype(jnp.bfloat16)
    layer_ref[...] = layer
    widened = layer.astype(jnp.float32)
    scale = lax.rsqrt(jnp.mean(widened * widened, axis=1, keepdims=True) + EPSILON)

    def table_rows(index):
        return pl.ds(pl.multiple_of(index * rows, rows), rows)

    table[table_rows(c), :] = (widened * scale * gain_ref[...]).astype(jnp.bfloat16)

    def row_copy(d, owner):
        return pltpu.make_async_remote_copy(
            src_ref=table.at[table_rows(owner), :],
            dst_ref=table.at[table_rows(owner), :],
            send_sem=row_send.at[d],
            recv_sem=row_recv.at[d],
            device_id=(e, lax.rem(c + d, ctx_count)),
            device_id_type=MESH,
        )

    for d in range(1, ctx_count):
        row_copy(d, c).start()
    for d in range(1, depth):
        relay_y(d)
    for d in range(depth):
        k_in(d, 0).wait_recv()
        k_in(d, 1).wait_recv()

    def project(owner):
        normed = table[table_rows(owner), :]
        for n in range(3):
            cols = slice(n * head_cols, (n + 1) * head_cols)
            proj[table_rows(owner), cols] = dot(normed, weights[:, cols]).astype(jnp.bfloat16)

    project(c)
    for d in range(1, ctx_count):
        owner = lax.rem(c + ctx_count - d, ctx_count)
        row_copy(d, owner).wait_recv()
        project(owner)

    total = table.shape[0]
    allowed = iota((total, total), 1) < count_ref[0]
    per_step = 128 // HEAD_DIM
    steps = head_cols // 128

    def out_copy(d, step):
        to = lax.rem(c + d, ctx_count)
        return pltpu.make_async_remote_copy(
            src_ref=away.at[table_rows(to), step * 128 : (step + 1) * 128],
            dst_ref=context_ref.at[
                :, pl.ds(pl.multiple_of(c * head_cols + step * 128, 128), 128)
            ],
            send_sem=out_send.at[d, step],
            recv_sem=out_recv.at[d, step],
            device_id=(e, to),
            device_id_type=MESH,
        )

    def out_in(d, step):
        source = lax.rem(c + ctx_count - d, ctx_count)
        cols = pl.ds(pl.multiple_of(source * head_cols + step * 128, 128), 128)
        return pltpu.make_async_remote_copy(
            src_ref=context_ref.at[:, cols],
            dst_ref=context_ref.at[:, cols],
            send_sem=out_send.at[d, step],
            recv_sem=out_recv.at[d, step],
            device_id=(e, source),
            device_id_type=MESH,
        )

    for step in range(steps):
        blended = []
        for h in range(step * per_step, (step + 1) * per_step):
            at = h * HEAD_DIM
            query = proj[:, at : at + HEAD_DIM]
            key = proj[:, head_cols + at : head_cols + at + HEAD_DIM]
            value = proj[:, 2 * head_cols + at : 2 * head_cols + at + HEAD_DIM]
            scores = dot_t(query, key, ((1,), (1,))) * (HEAD_DIM ** (-0.5))
            scores = jnp.where(allowed, scores, MASKED)
            top = jnp.max(scores, axis=1, keepdims=True)
            raw = jnp.where(allowed, jnp.exp(scores - top), 0.0)
            denominator = jnp.sum(raw, axis=1, keepdims=True)
            blended.append(dot(raw.astype(jnp.bfloat16), value) / denominator)
        away[:, step * 128 : (step + 1) * 128] = jnp.concatenate(blended, axis=1).astype(
            jnp.bfloat16
        )
        for d in range(1, ctx_count):
            out_copy(d, step).start()
        context_ref[:, pl.ds(pl.multiple_of(c * head_cols + step * 128, 128), 128)] = away[
            table_rows(c), step * 128 : (step + 1) * 128
        ]

    def wait_sends(d, carry):
        go_copy(d).wait_send()
        back_copy(d).wait_send()
        return carry

    lax.fori_loop(1, devices, wait_sends, 0)
    for d in range(1, depth):
        z_copy(d).wait_send()
    for d in range(depth):
        y_copy(d).wait_send()
        k_copy(d, 0).wait_send()
        k_copy(d, 1).wait_send()
    for d in range(1, ctx_count):
        gate_copy(d).wait_send()
        row_copy(d, c).wait_send()
        for step in range(steps):
            out_copy(d, step).wait_send()
            out_in(d, step).wait_recv()


def fused_local(*operands):
    inputs, selected, gate_weight, query_weight = (operands[i] for i in (0, 1, 3, 7))
    exp_count = lax.axis_size("exp")
    ctx_count = lax.axis_size("ctx")
    rows, width = inputs.shape
    local_experts, _, hidden = gate_weight.shape
    devices = exp_count * ctx_count
    block = local_experts * MOST * FOLD
    head_cols = width // ctx_count
    depth = exp_count // 4
    padded = local_experts * devices * MOST
    bf16 = jnp.bfloat16
    dma = pltpu.SemaphoreType.DMA
    vmem = pl.BlockSpec(memory_space=pltpu.VMEM)
    hbm = pl.BlockSpec(memory_space=pl.ANY)
    smem = pl.BlockSpec(memory_space=pltpu.SMEM)
    operands = operands[:6] + (operands[6].reshape(1, width),) + operands[7:]
    return pl.pallas_call(
        functools.partial(fused, exp_count, ctx_count),
        out_shape=(jax.ShapeDtypeStruct((rows, width), bf16),) * 2,
        in_specs=[vmem, vmem, vmem, hbm, hbm, hbm, vmem, hbm, hbm, hbm, smem],
        out_specs=(vmem, vmem),
        scratch_shapes=[
            pltpu.VMEM((local_experts, width, hidden), bf16),
            pltpu.VMEM((local_experts, width, hidden), bf16),
            pltpu.VMEM((local_experts, hidden, width), bf16),
            pltpu.VMEM((width, 3 * head_cols), bf16),
            pltpu.VMEM((exp_count * block, width // FOLD), bf16),
            pltpu.VMEM((devices * block, width // FOLD), bf16),
            pltpu.VMEM((devices * block, width // FOLD), bf16),
            pltpu.VMEM((devices * block, width // FOLD), bf16),
            pltpu.VMEM((ctx_count, padded, 128), jnp.float32),
            pltpu.VMEM((ctx_count * rows, width), bf16),
            pltpu.VMEM((ctx_count * rows, 3 * head_cols), bf16),
            pltpu.VMEM((ctx_count * rows, head_cols), bf16),
            pltpu.VMEM((devices * block, rows), bf16),
            dma((3 * local_experts,)),
            dma((3,)),
            dma((devices,)),
            dma((devices,)),
            dma((devices,)),
            dma((devices,)),
            dma((ctx_count,)),
            dma((ctx_count,)),
            dma((depth,)),
            dma((depth,)),
            dma((depth,)),
            dma((depth,)),
            dma((2 * depth,)),
            dma((2 * depth,)),
            dma((ctx_count,)),
            dma((ctx_count,)),
            dma((ctx_count, head_cols // 128)),
            dma((ctx_count, head_cols // 128)),
        ],
        compiler_params=pltpu.CompilerParams(
            collective_id=0, has_side_effects=True, vmem_limit_bytes=VMEM_LIMIT
        ),
    )(*operands)


def choose(*operands):
    inputs, gate_weight = operands[0], operands[3]
    exp_count, ctx_count = lax.axis_size("exp"), lax.axis_size("ctx")
    rows, width = inputs.shape
    local_experts = gate_weight.shape[0]
    devices = exp_count * ctx_count
    folded_rows = devices * local_experts * MOST * FOLD
    table = rows * ctx_count
    need = (
        3 * 2 * gate_weight.size
        + 6 * width * width // ctx_count
        + 8 * folded_rows * width // FOLD
        + 8 * FOLD * folded_rows * (folded_rows // FOLD)
        + 12 * table * table
    )
    ranks = max(2, (2 * operands[1].shape[1] + exp_count - 1) // exp_count)
    if exp_count % 4 == 0 and ranks == MOST and width // ctx_count % 128 == 0 and need < VMEM_LIMIT // 2:
        return fused_local(*operands)
    return local(*operands)


def solution(mesh):
    placed = (
        P(("exp", "ctx"), None),
        P(None, "ctx"),
        P("exp", "ctx"),
        P("exp", None, "ctx"),
        P("exp", None, "ctx"),
        P("exp", "ctx", None),
        P(),
        P("exp", None),
        P("exp", None),
        P("exp", None),
        P("exp"),
    )
    return jax.shard_map(
        choose,
        mesh=mesh,
        in_specs=placed,
        out_specs=(P(("exp", "ctx"), None), P(("exp", "ctx"), None)),
        check_vma=False,
    )
```

```python
import functools

import jax
import jax.numpy as jnp
from jax import lax
from jax.experimental import pallas as pl
from jax.experimental.pallas import tpu as pltpu
from jax.sharding import PartitionSpec as P

HEAD_DIM = 64


EPSILON = 1e-06
MASKED = -1e30


def block_rank(block_ids):
    slot_count = block_ids.shape[1]
    earlier = jnp.arange(slot_count)[:, None] > jnp.arange(slot_count)[None, :]
    same_block = block_ids[:, :, None] == block_ids[:, None, :]
    return jnp.sum(jnp.where(same_block & earlier[None], 1, 0), axis=2).astype(jnp.int32)


def local(
    inputs,
    selected,
    selection_gate,
    gate_weight,
    up_weight,
    down_weight,
    norm_gain,
    query_weight,
    key_weight,
    value_weight,
    train_count,
):
    exp_count = lax.axis_size("exp")
    ctx_count = lax.axis_size("ctx")
    exp_index = lax.axis_index("exp")
    ctx_index = lax.axis_index("ctx")
    row_count, model_width = inputs.shape
    expert_local = gate_weight.shape[0]
    group_take = selected.shape[1]
    most_rows = max(2, (2 * group_take + exp_count - 1) // exp_count)
    block_ids = selected // row_count
    slot_rank = block_rank(block_ids)
    own_block = exp_index * ctx_count + ctx_index
    is_mine = block_ids == own_block
    local_row = selected - own_block * row_count
    rank_slots = jnp.arange(most_rows, dtype=jnp.int32)
    slot_hit = is_mine[:, None, :] & (slot_rank[:, None, :] == rank_slots[None, :, None])
    pick_row = jnp.sum(jnp.where(slot_hit, local_row[:, None, :], 0), axis=2)
    filled = jnp.any(slot_hit, axis=2).reshape(-1)
    picked = jnp.take(inputs, pick_row.reshape(-1), axis=0)
    outgoing = jnp.where(filled[:, None], picked, jnp.zeros_like(picked)).reshape(
        exp_count, -1, model_width
    )
    incoming = lax.all_to_all(outgoing, "exp", split_axis=0, concat_axis=0, tiled=True)
    my_blocks = lax.dynamic_slice_in_dim(block_ids, exp_index * expert_local, expert_local, 0)
    my_rank = lax.dynamic_slice_in_dim(slot_rank, exp_index * expert_local, expert_local, 0)
    my_source = my_blocks // ctx_count
    expert_slot = jnp.arange(expert_local, dtype=jnp.int32)[:, None]
    flat_index = (my_source * expert_local + expert_slot) * most_rows + my_rank
    compact = jnp.take(incoming.reshape(-1, model_width), flat_index.T.reshape(-1), axis=0)
    compact = compact.reshape(group_take, expert_local, model_width)
    block_rows = lax.all_gather(compact, "ctx", axis=0, tiled=True)
    gate_part = jnp.einsum(
        "nxd,xdf->nxf", block_rows, gate_weight, preferred_element_type=jnp.float32
    )
    up_part = jnp.einsum("nxd,xdf->nxf", block_rows, up_weight, preferred_element_type=jnp.float32)
    hidden = (jax.nn.silu(gate_part) * up_part).astype(jnp.bfloat16)
    summed = lax.psum_scatter(
        jnp.einsum("nxf,xfd->nxd", hidden, down_weight, preferred_element_type=jnp.float32).astype(
            jnp.bfloat16
        ),
        "ctx",
        scatter_dimension=0,
        tiled=True,
    ).astype(jnp.float32)
    weighted = (summed * selection_gate.T[:, :, None]).astype(jnp.bfloat16)
    source_ids = jnp.arange(exp_count, dtype=jnp.int32)
    expert_ids = jnp.arange(expert_local, dtype=jnp.int32)[None, :, None, None]
    slot_index = jnp.arange(group_take, dtype=jnp.int32)[None, None, None, :]
    reply_hit = (my_source[None, :, None, :] == source_ids[:, None, None, None]) & (
        my_rank[None, :, None, :] == rank_slots[None, None, :, None]
    )
    reply_pick = jnp.sum(jnp.where(reply_hit, slot_index * expert_local + expert_ids, 0), axis=3)
    reply_filled = jnp.any(reply_hit, axis=3).reshape(-1)
    reply_rows = jnp.take(weighted.reshape(-1, model_width), reply_pick.reshape(-1), axis=0)
    reply_rows = jnp.where(reply_filled[:, None], reply_rows, jnp.zeros_like(reply_rows)).reshape(
        exp_count, -1, model_width
    )
    returned = lax.all_to_all(reply_rows, "exp", split_axis=0, concat_axis=0, tiled=True)
    owner_hit = (
        pick_row.reshape(-1)[None, :] == jnp.arange(row_count, dtype=jnp.int32)[:, None]
    ) & filled[None, :]
    moe_sum = jnp.dot(
        owner_hit.astype(jnp.bfloat16),
        returned.reshape(-1, model_width),
        preferred_element_type=jnp.float32,
    )
    layer_out = (inputs.astype(jnp.float32) + moe_sum).astype(jnp.bfloat16)
    widened = layer_out.astype(jnp.float32)
    scale_row = lax.rsqrt(jnp.mean(widened * widened, axis=1, keepdims=True) + EPSILON)
    normed = (widened * scale_row * norm_gain).astype(jnp.bfloat16)
    score_scale = HEAD_DIM ** (-0.5)
    train_rows = train_count[0]
    head_cols = model_width // ctx_count
    col_start = ctx_index * head_cols
    query_cols = lax.dynamic_slice_in_dim(query_weight, col_start, head_cols, 1)
    key_cols = lax.dynamic_slice_in_dim(key_weight, col_start, head_cols, 1)
    value_cols = lax.dynamic_slice_in_dim(value_weight, col_start, head_cols, 1)
    gathered = (
        lax.all_gather(query_cols, "exp", axis=0, tiled=True),
        lax.all_gather(key_cols, "exp", axis=0, tiled=True),
        lax.all_gather(value_cols, "exp", axis=0, tiled=True),
    )
    joined = jnp.concatenate(gathered, axis=1)
    table_proj = jnp.dot(
        lax.all_gather(normed, "ctx", axis=0, tiled=True),
        joined,
        preferred_element_type=jnp.float32,
    ).astype(jnp.bfloat16)
    table_count = table_proj.shape[0]
    local_heads = head_cols // HEAD_DIM
    query_all = table_proj[:, :head_cols].reshape(table_count, local_heads, HEAD_DIM)
    key_all = table_proj[:, head_cols : 2 * head_cols].reshape(table_count, local_heads, HEAD_DIM)
    value_all = table_proj[:, 2 * head_cols :].reshape(table_count, local_heads, HEAD_DIM)
    block_size = min(table_count, 512)
    allowed = jnp.arange(table_count, dtype=jnp.int32) < train_rows

    def attend_block(query_block):
        scores = (
            jnp.einsum("qhd,khd->hqk", query_block, key_all, preferred_element_type=jnp.float32)
            * score_scale
        )
        scores = jnp.where(allowed, scores, MASKED)
        top_score = jnp.max(scores, axis=2, keepdims=True)
        weights = jnp.where(allowed, jnp.exp(scores - top_score), 0.0)
        denominator = jnp.sum(weights, axis=2)
        blended = jnp.einsum(
            "hqk,khd->qhd",
            weights.astype(jnp.bfloat16),
            value_all,
            preferred_element_type=jnp.float32,
        )
        return (blended / denominator.T[:, :, None]).astype(jnp.bfloat16)

    head_context = lax.map(
        attend_block,
        query_all.reshape(table_count // block_size, block_size, local_heads, HEAD_DIM),
    )
    context = lax.all_to_all(
        head_context.reshape(table_count, head_cols), "ctx", split_axis=0, concat_axis=1, tiled=True
    )
    return (layer_out, context)


MESH = pl.DeviceIdType.MESH
MOST = 2
FOLD = 4
NEVER = 1 << 20
VMEM_LIMIT = 60 * 1024 * 1024


def iota(shape, dim):
    return lax.broadcasted_iota(jnp.int32, shape, dim)


def onehot(condition):
    return jnp.where(condition, 1.0, 0.0).astype(jnp.bfloat16)


def dot(a, b):
    return jnp.dot(a, b, preferred_element_type=jnp.float32)


def dot_t(a, b, contract):
    return lax.dot_general(a, b, (contract, ((), ())), preferred_element_type=jnp.float32)


def fused(
    exp_count,
    ctx_count,
    x_ref,
    sel_ref,
    gate_ref,
    wg_hbm,
    wu_hbm,
    wd_hbm,
    gain_ref,
    q_hbm,
    k_hbm,
    v_hbm,
    count_ref,
    layer_ref,
    context_ref,
    wg,
    wu,
    wd,
    weights,
    out_rows,
    in_rows,
    reply_rows,
    back_rows,
    gates,
    table,
    proj,
    away,
    spread,
    hbm_sem,
    col_sem,
    go_send,
    go_recv,
    back_send,
    back_recv,
    gate_send,
    gate_recv,
    z_send,
    z_recv,
    y_send,
    y_recv,
    c_send,
    c_recv,
    row_send,
    row_recv,
    out_send,
    out_recv,
):
    e = lax.axis_index("exp")
    c = lax.axis_index("ctx")
    rows, width = x_ref.shape
    take, experts = sel_ref.shape
    local_experts = wg.shape[0]
    devices = exp_count * ctx_count
    me = e * ctx_count + c
    group = local_experts * MOST
    block = group * FOLD
    fold = width // FOLD
    shard = q_hbm.shape[0]
    head_cols = width // ctx_count
    padded = local_experts * devices * MOST

    barrier = pltpu.get_barrier_semaphore()

    def greet(d, carry):
        to = lax.rem(me + d, devices)
        pl.semaphore_signal(
            barrier, inc=1, device_id=(to // ctx_count, lax.rem(to, ctx_count)), device_id_type=MESH
        )
        return carry

    lax.fori_loop(1, devices, greet, 0)

    def rows_of(o):
        return weights.at[pl.ds(pl.multiple_of(o * shard, shard), shard), :]

    own_cols = []
    for n, ref in enumerate((q_hbm, k_hbm, v_hbm)):
        copy = pltpu.make_async_copy(
            ref.at[:, pl.ds(pl.multiple_of(c * head_cols, head_cols), head_cols)],
            weights.at[
                pl.ds(pl.multiple_of(e * shard, shard), shard), pl.ds(n * head_cols, head_cols)
            ],
            col_sem.at[n],
        )
        copy.start()
        own_cols.append(copy)
    loads = []
    for x in range(local_experts):
        for n, (hbm, vmem) in enumerate(((wg_hbm, wg), (wu_hbm, wu), (wd_hbm, wd))):
            copy = pltpu.make_async_copy(hbm.at[x], vmem.at[x], hbm_sem.at[x * 3 + n])
            copy.start()
            loads.append(copy)

    selected = sel_ref[...]
    start = me * rows
    mine = (selected >= start) & (selected < start + rows)
    offset = selected - start
    low = jnp.min(jnp.where(mine, offset, NEVER), axis=0, keepdims=True)
    high = jnp.max(jnp.where(mine, offset, -1), axis=0, keepdims=True)
    high = jnp.where(high == low, NEVER, high)
    down = iota((rows, experts), 0)
    picks = (onehot(down == low), onehot(down == high))

    def taker(m, per_expert_device):
        return m // (block * per_expert_device) * local_experts + lax.rem(m, group) // MOST

    out_count = exp_count * block
    m = iota((out_count, experts), 0)
    hit = iota((out_count, experts), 1) == taker(m, 1)
    source = sum(
        dot_t(onehot(hit & (lax.rem(m, MOST) == n)), picks[n], ((1,), (1,))) for n in range(MOST)
    )
    everything = dot(source.astype(jnp.bfloat16), x_ref[...])
    part = lax.rem(iota((out_count, 1), 0), block) // group
    folded = jnp.zeros((out_count, fold), jnp.float32)
    for f in range(FOLD):
        folded = jnp.where(part == f, everything[:, f * fold : (f + 1) * fold], folded)
    out_rows[...] = folded.astype(jnp.bfloat16)

    in_count = devices * block
    m = iota((experts, in_count), 1)
    hit = iota((experts, in_count), 0) == taker(m, ctx_count)
    spread[...] = sum(
        dot(picks[n], onehot(hit & (lax.rem(m, MOST) == n))) for n in range(MOST)
    ).astype(jnp.bfloat16)

    pair = iota((devices * MOST, 1), 0)
    owner = pair // MOST
    rank = lax.rem(pair, MOST)
    for x in range(local_experts):
        at_x = iota((take, experts), 1) == e * local_experts + x
        column = jnp.sum(jnp.where(at_x, selected, 0), axis=1, keepdims=True)
        same = iota((take, take), 0) == iota((take, take), 1)
        sel_x = jnp.sum(jnp.where(same, column, 0), axis=0, keepdims=True)
        gate_x = gate_ref[pl.ds(x, 1), :]
        off = jnp.broadcast_to(sel_x, (devices * MOST, take)) - owner * rows
        own = (off >= 0) & (off < rows) & (lax.rem(owner, ctx_count) == c)
        lo = jnp.min(jnp.where(own, off, NEVER), axis=1, keepdims=True)
        hi = jnp.max(jnp.where(own, off, -1), axis=1, keepdims=True)
        want = jnp.where(rank == 0, lo, jnp.where(hi == lo, NEVER, hi))
        value = jnp.sum(
            jnp.where(own & (off == want), jnp.broadcast_to(gate_x, off.shape), 0.0),
            axis=1,
            keepdims=True,
        )
        gates[0, x * devices * MOST : (x + 1) * devices * MOST, :] = jnp.broadcast_to(
            value, (devices * MOST, gates.shape[2])
        )

    def slot(ref, index):
        return ref.at[pl.ds(pl.multiple_of(index * block, block), block), :]

    def go_copy(d):
        to = lax.rem(me + d, devices)
        return pltpu.make_async_remote_copy(
            src_ref=slot(out_rows, to // ctx_count),
            dst_ref=slot(in_rows, me),
            send_sem=go_send.at[d],
            recv_sem=go_recv.at[d],
            device_id=(to // ctx_count, lax.rem(to, ctx_count)),
            device_id_type=MESH,
        )

    def back_copy(d):
        to = lax.rem(me + d, devices)
        return pltpu.make_async_remote_copy(
            src_ref=slot(reply_rows, to),
            dst_ref=slot(back_rows, me),
            send_sem=back_send.at[d],
            recv_sem=back_recv.at[d],
            device_id=(to // ctx_count, lax.rem(to, ctx_count)),
            device_id_type=MESH,
        )

    def arrived(ref, sems, d):
        source = lax.rem(me + devices - d, devices)
        pltpu.make_async_remote_copy(
            src_ref=slot(ref, source),
            dst_ref=slot(ref, source),
            send_sem=sems.at[d],
            recv_sem=sems.at[d],
            device_id=(source // ctx_count, lax.rem(source, ctx_count)),
            device_id_type=MESH,
        ).wait_recv()

    def gate_copy(d):
        return pltpu.make_async_remote_copy(
            src_ref=gates.at[0],
            dst_ref=gates.at[d],
            send_sem=gate_send.at[d],
            recv_sem=gate_recv.at[d],
            device_id=(e, lax.rem(c + d, ctx_count)),
            device_id_type=MESH,
        )

    depth = exp_count // 4
    z, y, k = e // 4, lax.rem(e // 2, 2), lax.rem(e, 2)

    def member(z_at, y_at, k_at):
        return z_at * 4 + y_at * 2 + k_at

    def weight_copy(o, to, send, recv):
        return pltpu.make_async_remote_copy(
            src_ref=rows_of(o),
            dst_ref=rows_of(o),
            send_sem=send,
            recv_sem=recv,
            device_id=(to, c),
            device_id_type=MESH,
        )

    y_peer = member(z, 1 - y, k)
    k_peer = member(z, y, 1 - k)

    def z_copy(d):
        return weight_copy(e, member(lax.rem(z + d, depth), y, k), z_send.at[d], z_recv.at[d])

    def behind(d):
        return lax.rem(z + depth - d, depth)

    def y_copy(d):
        return weight_copy(member(behind(d), y, k), y_peer, y_send.at[d], y_recv.at[d])

    def y_in(d):
        return weight_copy(member(behind(d), 1 - y, k), y_peer, y_send.at[d], y_recv.at[d])

    def z_in(d):
        return weight_copy(member(behind(d), y, k), y_peer, z_send.at[d], z_recv.at[d])

    def k_copy(d, across):
        y_at = 1 - y if across else y
        n = d + depth * across
        return weight_copy(member(behind(d), y_at, k), k_peer, c_send.at[n], c_recv.at[n])

    def k_in(d, across):
        y_at = 1 - y if across else y
        n = d + depth * across
        return weight_copy(member(behind(d), y_at, 1 - k), k_peer, c_send.at[n], c_recv.at[n])

    def relay_z(d):
        z_in(d).wait_recv()
        y_copy(d).start()
        k_copy(d, 0).start()

    def relay_y(d):
        y_in(d).wait_recv()
        k_copy(d, 1).start()

    pl.semaphore_wait(barrier, devices - 1)

    def start_go(d, carry):
        go_copy(d).start()
        return carry

    lax.fori_loop(1, devices, start_go, 0)
    for d in range(1, ctx_count):
        gate_copy(d).start()
    for copy in own_cols:
        copy.wait()
    for d in range(1, depth):
        z_copy(d).start()
    y_copy(0).start()
    k_copy(0, 0).start()

    in_rows[pl.ds(pl.multiple_of(me * block, block), block), :] = out_rows[
        pl.ds(pl.multiple_of(e * block, block), block), :
    ]
    m = iota((padded, in_count), 1)
    n = iota((padded, in_count), 0)
    per = devices * MOST
    matches = (
        (m // block == lax.rem(n, per) // MOST)
        & (lax.rem(m, group) // MOST == n // per)
        & (lax.rem(m, MOST) == lax.rem(n, MOST))
    )
    unfold = [
        onehot(matches & (lax.rem(m, block) // group == f)) for f in range(FOLD)
    ]

    def wait_go(d, carry):
        arrived(in_rows, go_recv, d)
        return carry

    lax.fori_loop(1, devices, wait_go, 0)
    received = in_rows[...]
    tokens = jnp.concatenate(
        [dot(u, received).astype(jnp.bfloat16) for u in unfold], axis=1
    )
    for d in range(1, ctx_count):
        gate_copy(d).wait_recv()
    parts = []
    for x in range(local_experts):
        chosen = tokens[x * per : (x + 1) * per, :]
        loads[3 * x].wait()
        gate_part = dot(chosen, wg[x])
        loads[3 * x + 1].wait()
        up_part = dot(chosen, wu[x])
        hidden = (gate_part / (1.0 + jnp.exp(-gate_part)) * up_part).astype(jnp.bfloat16)
        loads[3 * x + 2].wait()
        expert_out = dot(hidden, wd[x])
        factor = gates[0, x * per : (x + 1) * per, 0:1]
        for d in range(1, ctx_count):
            factor = factor + gates[d, x * per : (x + 1) * per, 0:1]
        parts.append((expert_out * factor).astype(jnp.bfloat16))
        if x == 0:
            relay_y(0)
            for d in range(1, min(2, depth)):
                relay_z(d)
    weighted = jnp.concatenate(parts, axis=0)
    m = iota((in_count, padded), 0)
    n = iota((in_count, padded), 1)
    back = onehot(
        (m // block == lax.rem(n, per) // MOST)
        & (lax.rem(m, group) // MOST == n // per)
        & (lax.rem(m, MOST) == lax.rem(n, MOST))
    )
    part = lax.rem(iota((in_count, 1), 0), block) // group
    folded = jnp.zeros((in_count, fold), jnp.float32)
    for f in range(FOLD):
        folded = jnp.where(part == f, dot(back, weighted[:, f * fold : (f + 1) * fold]), folded)
    reply_rows[...] = folded.astype(jnp.bfloat16)

    def start_back(d, carry):
        back_copy(d).start()
        return carry

    lax.fori_loop(1, devices, start_back, 0)
    back_rows[pl.ds(pl.multiple_of(me * block, block), block), :] = reply_rows[
        pl.ds(pl.multiple_of(me * block, block), block), :
    ]
    for d in range(2, depth):
        relay_z(d)

    def wait_back(d, carry):
        arrived(back_rows, back_recv, d)
        return carry

    lax.fori_loop(1, devices, wait_back, 0)
    returned = back_rows[...]
    along = lax.rem(iota((rows, in_count), 1), block) // group
    moe = []
    for f in range(FOLD):
        hits = jnp.where(along == f, spread[...], jnp.zeros_like(spread[...]))
        moe.append(dot(hits, returned))
    layer = (x_ref[...].astype(jnp.float32) + jnp.concatenate(moe, axis=1)).astype(jnp.bfloat16)
    layer_ref[...] = layer
    widened = layer.astype(jnp.float32)
    scale = lax.rsqrt(jnp.mean(widened * widened, axis=1, keepdims=True) + EPSILON)

    def table_rows(index):
        return pl.ds(pl.multiple_of(index * rows, rows), rows)

    table[table_rows(c), :] = (widened * scale * gain_ref[...]).astype(jnp.bfloat16)

    def row_copy(d, owner):
        return pltpu.make_async_remote_copy(
            src_ref=table.at[table_rows(owner), :],
            dst_ref=table.at[table_rows(owner), :],
            send_sem=row_send.at[d],
            recv_sem=row_recv.at[d],
            device_id=(e, lax.rem(c + d, ctx_count)),
            device_id_type=MESH,
        )

    for d in range(1, ctx_count):
        row_copy(d, c).start()
    for d in range(1, depth):
        relay_y(d)
    for d in range(depth):
        k_in(d, 0).wait_recv()
        k_in(d, 1).wait_recv()

    def project(owner):
        normed = table[table_rows(owner), :]
        for n in range(3):
            cols = slice(n * head_cols, (n + 1) * head_cols)
            proj[table_rows(owner), cols] = dot(normed, weights[:, cols]).astype(jnp.bfloat16)

    project(c)
    for d in range(1, ctx_count):
        owner = lax.rem(c + ctx_count - d, ctx_count)
        row_copy(d, owner).wait_recv()
        project(owner)

    total = table.shape[0]
    allowed = iota((total, total), 1) < count_ref[0]
    per_step = 128 // HEAD_DIM
    steps = head_cols // 128

    def out_copy(d, step):
        to = lax.rem(c + d, ctx_count)
        return pltpu.make_async_remote_copy(
            src_ref=away.at[table_rows(to), step * 128 : (step + 1) * 128],
            dst_ref=context_ref.at[
                :, pl.ds(pl.multiple_of(c * head_cols + step * 128, 128), 128)
            ],
            send_sem=out_send.at[d, step],
            recv_sem=out_recv.at[d, step],
            device_id=(e, to),
            device_id_type=MESH,
        )

    def out_in(d, step):
        source = lax.rem(c + ctx_count - d, ctx_count)
        cols = pl.ds(pl.multiple_of(source * head_cols + step * 128, 128), 128)
        return pltpu.make_async_remote_copy(
            src_ref=context_ref.at[:, cols],
            dst_ref=context_ref.at[:, cols],
            send_sem=out_send.at[d, step],
            recv_sem=out_recv.at[d, step],
            device_id=(e, source),
            device_id_type=MESH,
        )

    for step in range(steps):
        blended = []
        for h in range(step * per_step, (step + 1) * per_step):
            at = h * HEAD_DIM
            query = proj[:, at : at + HEAD_DIM]
            key = proj[:, head_cols + at : head_cols + at + HEAD_DIM]
            value = proj[:, 2 * head_cols + at : 2 * head_cols + at + HEAD_DIM]
            scores = dot_t(query, key, ((1,), (1,))) * (HEAD_DIM ** (-0.5))
            scores = jnp.where(allowed, scores, MASKED)
            top = jnp.max(scores, axis=1, keepdims=True)
            raw = jnp.where(allowed, jnp.exp(scores - top), 0.0)
            denominator = jnp.sum(raw, axis=1, keepdims=True)
            blended.append(dot(raw.astype(jnp.bfloat16), value) / denominator)
        away[:, step * 128 : (step + 1) * 128] = jnp.concatenate(blended, axis=1).astype(
            jnp.bfloat16
        )
        for d in range(1, ctx_count):
            out_copy(d, step).start()
        context_ref[:, pl.ds(pl.multiple_of(c * head_cols + step * 128, 128), 128)] = away[
            table_rows(c), step * 128 : (step + 1) * 128
        ]

    def wait_sends(d, carry):
        go_copy(d).wait_send()
        back_copy(d).wait_send()
        return carry

    lax.fori_loop(1, devices, wait_sends, 0)
    for d in range(1, depth):
        z_copy(d).wait_send()
    for d in range(depth):
        y_copy(d).wait_send()
        k_copy(d, 0).wait_send()
        k_copy(d, 1).wait_send()
    for d in range(1, ctx_count):
        gate_copy(d).wait_send()
        row_copy(d, c).wait_send()
        for step in range(steps):
            out_copy(d, step).wait_send()
            out_in(d, step).wait_recv()


def emit(layer_ref, context_ref, layer_out, context_out, sem):
    copies = [
        pltpu.make_async_copy(layer_ref, layer_out, sem.at[0]),
        pltpu.make_async_copy(context_ref, context_out, sem.at[1]),
    ]
    for copy in copies:
        copy.start()
    for copy in copies:
        copy.wait()


def fused_local(*operands):
    inputs, selected, gate_weight, query_weight = (operands[i] for i in (0, 1, 3, 7))
    exp_count = lax.axis_size("exp")
    ctx_count = lax.axis_size("ctx")
    rows, width = inputs.shape
    local_experts, _, hidden = gate_weight.shape
    devices = exp_count * ctx_count
    block = local_experts * MOST * FOLD
    head_cols = width // ctx_count
    depth = exp_count // 4
    padded = local_experts * devices * MOST
    bf16 = jnp.bfloat16
    dma = pltpu.SemaphoreType.DMA
    vmem = pl.BlockSpec(memory_space=pltpu.VMEM)
    hbm = pl.BlockSpec(memory_space=pl.ANY)
    smem = pl.BlockSpec(memory_space=pltpu.SMEM)
    operands = operands[:1] + (operands[1].T,) + operands[2:6] + (operands[6].reshape(1, width),) + operands[7:]
    results = pl.pallas_call(
        functools.partial(fused, exp_count, ctx_count),
        out_shape=(jax.ShapeDtypeStruct((rows, width), bf16),) * 2,
        in_specs=[vmem, vmem, vmem, hbm, hbm, hbm, vmem, hbm, hbm, hbm, smem],
        out_specs=(vmem, vmem),
        scratch_shapes=[
            pltpu.VMEM((local_experts, width, hidden), bf16),
            pltpu.VMEM((local_experts, width, hidden), bf16),
            pltpu.VMEM((local_experts, hidden, width), bf16),
            pltpu.VMEM((width, 3 * head_cols), bf16),
            pltpu.VMEM((exp_count * block, width // FOLD), bf16),
            pltpu.VMEM((devices * block, width // FOLD), bf16),
            pltpu.VMEM((devices * block, width // FOLD), bf16),
            pltpu.VMEM((devices * block, width // FOLD), bf16),
            pltpu.VMEM((ctx_count, padded, 128), jnp.float32),
            pltpu.VMEM((ctx_count * rows, width), bf16),
            pltpu.VMEM((ctx_count * rows, 3 * head_cols), bf16),
            pltpu.VMEM((ctx_count * rows, head_cols), bf16),
            pltpu.VMEM((rows, devices * block), bf16),
            dma((3 * local_experts,)),
            dma((3,)),
            dma((devices,)),
            dma((devices,)),
            dma((devices,)),
            dma((devices,)),
            dma((ctx_count,)),
            dma((ctx_count,)),
            dma((depth,)),
            dma((depth,)),
            dma((depth,)),
            dma((depth,)),
            dma((2 * depth,)),
            dma((2 * depth,)),
            dma((ctx_count,)),
            dma((ctx_count,)),
            dma((ctx_count, head_cols // 128)),
            dma((ctx_count, head_cols // 128)),
        ],
        compiler_params=pltpu.CompilerParams(
            collective_id=0, has_side_effects=True, vmem_limit_bytes=VMEM_LIMIT
        ),
    )(*operands)
    return pl.pallas_call(
        emit,
        out_shape=(jax.ShapeDtypeStruct((rows, width), bf16),) * 2,
        in_specs=[vmem, vmem],
        out_specs=(hbm, hbm),
        scratch_shapes=[dma((2,))],
    )(*results)


def choose(*operands):
    inputs, gate_weight = operands[0], operands[3]
    exp_count, ctx_count = lax.axis_size("exp"), lax.axis_size("ctx")
    rows, width = inputs.shape
    local_experts = gate_weight.shape[0]
    devices = exp_count * ctx_count
    folded_rows = devices * local_experts * MOST * FOLD
    table = rows * ctx_count
    need = (
        3 * 2 * gate_weight.size
        + 6 * width * width // ctx_count
        + 8 * folded_rows * width // FOLD
        + 8 * FOLD * folded_rows * (folded_rows // FOLD)
        + 12 * table * table
    )
    ranks = max(2, (2 * operands[1].shape[1] + exp_count - 1) // exp_count)
    if exp_count % 4 == 0 and ranks == MOST and width // ctx_count % 128 == 0 and need < VMEM_LIMIT // 2:
        return fused_local(*operands)
    return local(*operands)


def solution(mesh):
    placed = (
        P(("exp", "ctx"), None),
        P(None, "ctx"),
        P("exp", "ctx"),
        P("exp", None, "ctx"),
        P("exp", None, "ctx"),
        P("exp", "ctx", None),
        P(),
        P("exp", None),
        P("exp", None),
        P("exp", None),
        P("exp"),
    )
    return jax.shard_map(
        choose,
        mesh=mesh,
        in_specs=placed,
        out_specs=(P(("exp", "ctx"), None), P(("exp", "ctx"), None)),
        check_vma=False,
    )
```

```python
import functools

import jax
import jax.numpy as jnp
from jax import lax
from jax.experimental import pallas as pl
from jax.experimental.pallas import tpu as pltpu
from jax.sharding import PartitionSpec as P

HEAD_DIM = 64


EPSILON = 1e-06
MASKED = -1e30


def block_rank(block_ids):
    slot_count = block_ids.shape[1]
    earlier = jnp.arange(slot_count)[:, None] > jnp.arange(slot_count)[None, :]
    same_block = block_ids[:, :, None] == block_ids[:, None, :]
    return jnp.sum(jnp.where(same_block & earlier[None], 1, 0), axis=2).astype(jnp.int32)


def local(
    inputs,
    selected,
    selection_gate,
    gate_weight,
    up_weight,
    down_weight,
    norm_gain,
    query_weight,
    key_weight,
    value_weight,
    train_count,
):
    exp_count = lax.axis_size("exp")
    ctx_count = lax.axis_size("ctx")
    exp_index = lax.axis_index("exp")
    ctx_index = lax.axis_index("ctx")
    row_count, model_width = inputs.shape
    expert_local = gate_weight.shape[0]
    group_take = selected.shape[1]
    most_rows = max(2, (2 * group_take + exp_count - 1) // exp_count)
    block_ids = selected // row_count
    slot_rank = block_rank(block_ids)
    own_block = exp_index * ctx_count + ctx_index
    is_mine = block_ids == own_block
    local_row = selected - own_block * row_count
    rank_slots = jnp.arange(most_rows, dtype=jnp.int32)
    slot_hit = is_mine[:, None, :] & (slot_rank[:, None, :] == rank_slots[None, :, None])
    pick_row = jnp.sum(jnp.where(slot_hit, local_row[:, None, :], 0), axis=2)
    filled = jnp.any(slot_hit, axis=2).reshape(-1)
    picked = jnp.take(inputs, pick_row.reshape(-1), axis=0)
    outgoing = jnp.where(filled[:, None], picked, jnp.zeros_like(picked)).reshape(
        exp_count, -1, model_width
    )
    incoming = lax.all_to_all(outgoing, "exp", split_axis=0, concat_axis=0, tiled=True)
    my_blocks = lax.dynamic_slice_in_dim(block_ids, exp_index * expert_local, expert_local, 0)
    my_rank = lax.dynamic_slice_in_dim(slot_rank, exp_index * expert_local, expert_local, 0)
    my_source = my_blocks // ctx_count
    expert_slot = jnp.arange(expert_local, dtype=jnp.int32)[:, None]
    flat_index = (my_source * expert_local + expert_slot) * most_rows + my_rank
    compact = jnp.take(incoming.reshape(-1, model_width), flat_index.T.reshape(-1), axis=0)
    compact = compact.reshape(group_take, expert_local, model_width)
    block_rows = lax.all_gather(compact, "ctx", axis=0, tiled=True)
    gate_part = jnp.einsum(
        "nxd,xdf->nxf", block_rows, gate_weight, preferred_element_type=jnp.float32
    )
    up_part = jnp.einsum("nxd,xdf->nxf", block_rows, up_weight, preferred_element_type=jnp.float32)
    hidden = (jax.nn.silu(gate_part) * up_part).astype(jnp.bfloat16)
    summed = lax.psum_scatter(
        jnp.einsum("nxf,xfd->nxd", hidden, down_weight, preferred_element_type=jnp.float32).astype(
            jnp.bfloat16
        ),
        "ctx",
        scatter_dimension=0,
        tiled=True,
    ).astype(jnp.float32)
    weighted = (summed * selection_gate.T[:, :, None]).astype(jnp.bfloat16)
    source_ids = jnp.arange(exp_count, dtype=jnp.int32)
    expert_ids = jnp.arange(expert_local, dtype=jnp.int32)[None, :, None, None]
    slot_index = jnp.arange(group_take, dtype=jnp.int32)[None, None, None, :]
    reply_hit = (my_source[None, :, None, :] == source_ids[:, None, None, None]) & (
        my_rank[None, :, None, :] == rank_slots[None, None, :, None]
    )
    reply_pick = jnp.sum(jnp.where(reply_hit, slot_index * expert_local + expert_ids, 0), axis=3)
    reply_filled = jnp.any(reply_hit, axis=3).reshape(-1)
    reply_rows = jnp.take(weighted.reshape(-1, model_width), reply_pick.reshape(-1), axis=0)
    reply_rows = jnp.where(reply_filled[:, None], reply_rows, jnp.zeros_like(reply_rows)).reshape(
        exp_count, -1, model_width
    )
    returned = lax.all_to_all(reply_rows, "exp", split_axis=0, concat_axis=0, tiled=True)
    owner_hit = (
        pick_row.reshape(-1)[None, :] == jnp.arange(row_count, dtype=jnp.int32)[:, None]
    ) & filled[None, :]
    moe_sum = jnp.dot(
        owner_hit.astype(jnp.bfloat16),
        returned.reshape(-1, model_width),
        preferred_element_type=jnp.float32,
    )
    layer_out = (inputs.astype(jnp.float32) + moe_sum).astype(jnp.bfloat16)
    widened = layer_out.astype(jnp.float32)
    scale_row = lax.rsqrt(jnp.mean(widened * widened, axis=1, keepdims=True) + EPSILON)
    normed = (widened * scale_row * norm_gain).astype(jnp.bfloat16)
    score_scale = HEAD_DIM ** (-0.5)
    train_rows = train_count[0]
    head_cols = model_width // ctx_count
    col_start = ctx_index * head_cols
    query_cols = lax.dynamic_slice_in_dim(query_weight, col_start, head_cols, 1)
    key_cols = lax.dynamic_slice_in_dim(key_weight, col_start, head_cols, 1)
    value_cols = lax.dynamic_slice_in_dim(value_weight, col_start, head_cols, 1)
    gathered = (
        lax.all_gather(query_cols, "exp", axis=0, tiled=True),
        lax.all_gather(key_cols, "exp", axis=0, tiled=True),
        lax.all_gather(value_cols, "exp", axis=0, tiled=True),
    )
    joined = jnp.concatenate(gathered, axis=1)
    table_proj = jnp.dot(
        lax.all_gather(normed, "ctx", axis=0, tiled=True),
        joined,
        preferred_element_type=jnp.float32,
    ).astype(jnp.bfloat16)
    table_count = table_proj.shape[0]
    local_heads = head_cols // HEAD_DIM
    query_all = table_proj[:, :head_cols].reshape(table_count, local_heads, HEAD_DIM)
    key_all = table_proj[:, head_cols : 2 * head_cols].reshape(table_count, local_heads, HEAD_DIM)
    value_all = table_proj[:, 2 * head_cols :].reshape(table_count, local_heads, HEAD_DIM)
    block_size = min(table_count, 512)
    allowed = jnp.arange(table_count, dtype=jnp.int32) < train_rows

    def attend_block(query_block):
        scores = (
            jnp.einsum("qhd,khd->hqk", query_block, key_all, preferred_element_type=jnp.float32)
            * score_scale
        )
        scores = jnp.where(allowed, scores, MASKED)
        top_score = jnp.max(scores, axis=2, keepdims=True)
        weights = jnp.where(allowed, jnp.exp(scores - top_score), 0.0)
        denominator = jnp.sum(weights, axis=2)
        blended = jnp.einsum(
            "hqk,khd->qhd",
            weights.astype(jnp.bfloat16),
            value_all,
            preferred_element_type=jnp.float32,
        )
        return (blended / denominator.T[:, :, None]).astype(jnp.bfloat16)

    head_context = lax.map(
        attend_block,
        query_all.reshape(table_count // block_size, block_size, local_heads, HEAD_DIM),
    )
    context = lax.all_to_all(
        head_context.reshape(table_count, head_cols), "ctx", split_axis=0, concat_axis=1, tiled=True
    )
    return (layer_out, context)


MESH = pl.DeviceIdType.MESH
MOST = 2
FOLD = 4
NEVER = 1 << 20
VMEM_LIMIT = 60 * 1024 * 1024


def iota(shape, dim):
    return lax.broadcasted_iota(jnp.int32, shape, dim)


def onehot(condition):
    return jnp.where(condition, 1.0, 0.0).astype(jnp.bfloat16)


def dot(a, b):
    return jnp.dot(a, b, preferred_element_type=jnp.float32)


def dot_t(a, b, contract):
    return lax.dot_general(a, b, (contract, ((), ())), preferred_element_type=jnp.float32)


def fused(
    exp_count,
    ctx_count,
    x_ref,
    sel_ref,
    gate_ref,
    wg_hbm,
    wu_hbm,
    wd_hbm,
    gain_ref,
    q_hbm,
    k_hbm,
    v_hbm,
    count_ref,
    layer_ref,
    context_ref,
    wg,
    wu,
    wd,
    weights,
    out_rows,
    in_rows,
    reply_rows,
    back_rows,
    gates,
    table,
    proj,
    away,
    spread,
    hbm_sem,
    col_sem,
    go_send,
    go_recv,
    back_send,
    back_recv,
    gate_send,
    gate_recv,
    z_send,
    z_recv,
    y_send,
    y_recv,
    c_send,
    c_recv,
    row_send,
    row_recv,
    out_send,
    out_recv,
):
    e = lax.axis_index("exp")
    c = lax.axis_index("ctx")
    rows, width = x_ref.shape
    take, experts = sel_ref.shape
    local_experts = wg.shape[0]
    devices = exp_count * ctx_count
    me = e * ctx_count + c
    group = local_experts * MOST
    block = group * FOLD
    fold = width // FOLD
    shard = q_hbm.shape[0]
    head_cols = width // ctx_count
    padded = local_experts * devices * MOST

    barrier = pltpu.get_barrier_semaphore()

    def greet(d, carry):
        to = lax.rem(me + d, devices)
        pl.semaphore_signal(
            barrier, inc=1, device_id=(to // ctx_count, lax.rem(to, ctx_count)), device_id_type=MESH
        )
        return carry

    lax.fori_loop(1, devices, greet, 0)

    def rows_of(o):
        return weights.at[pl.ds(pl.multiple_of(o * shard, shard), shard), :]

    own_cols = []
    for n, ref in enumerate((q_hbm, k_hbm, v_hbm)):
        copy = pltpu.make_async_copy(
            ref.at[:, pl.ds(pl.multiple_of(c * head_cols, head_cols), head_cols)],
            weights.at[
                pl.ds(pl.multiple_of(e * shard, shard), shard), pl.ds(n * head_cols, head_cols)
            ],
            col_sem.at[n],
        )
        copy.start()
        own_cols.append(copy)
    loads = []
    for x in range(local_experts):
        for n, (hbm, vmem) in enumerate(((wg_hbm, wg), (wu_hbm, wu), (wd_hbm, wd))):
            copy = pltpu.make_async_copy(hbm.at[x], vmem.at[x], hbm_sem.at[x * 3 + n])
            copy.start()
            loads.append(copy)

    selected = sel_ref[...]
    start = me * rows
    mine = (selected >= start) & (selected < start + rows)
    offset = selected - start
    low = jnp.min(jnp.where(mine, offset, NEVER), axis=0, keepdims=True)
    high = jnp.max(jnp.where(mine, offset, -1), axis=0, keepdims=True)
    high = jnp.where(high == low, NEVER, high)
    down = iota((rows, experts), 0)
    picks = (onehot(down == low), onehot(down == high))

    def taker(m, per_expert_device):
        return m // (block * per_expert_device) * local_experts + lax.rem(m, group) // MOST

    out_count = exp_count * block
    m = iota((out_count, experts), 0)
    hit = iota((out_count, experts), 1) == taker(m, 1)
    source = sum(
        dot_t(onehot(hit & (lax.rem(m, MOST) == n)), picks[n], ((1,), (1,))) for n in range(MOST)
    )
    everything = dot(source.astype(jnp.bfloat16), x_ref[...])
    part = lax.rem(iota((out_count, 1), 0), block) // group
    folded = jnp.zeros((out_count, fold), jnp.float32)
    for f in range(FOLD):
        folded = jnp.where(part == f, everything[:, f * fold : (f + 1) * fold], folded)
    out_rows[...] = folded.astype(jnp.bfloat16)

    in_count = devices * block
    m = iota((experts, in_count), 1)
    hit = iota((experts, in_count), 0) == taker(m, ctx_count)
    spread[...] = sum(
        dot(picks[n], onehot(hit & (lax.rem(m, MOST) == n))) for n in range(MOST)
    ).astype(jnp.bfloat16)

    pair = iota((devices * MOST, 1), 0)
    owner = pair // MOST
    rank = lax.rem(pair, MOST)
    for x in range(local_experts):
        at_x = iota((take, experts), 1) == e * local_experts + x
        column = jnp.sum(jnp.where(at_x, selected, 0), axis=1, keepdims=True)
        same = iota((take, take), 0) == iota((take, take), 1)
        sel_x = jnp.sum(jnp.where(same, column, 0), axis=0, keepdims=True)
        gate_x = gate_ref[pl.ds(x, 1), :]
        off = jnp.broadcast_to(sel_x, (devices * MOST, take)) - owner * rows
        own = (off >= 0) & (off < rows) & (lax.rem(owner, ctx_count) == c)
        lo = jnp.min(jnp.where(own, off, NEVER), axis=1, keepdims=True)
        hi = jnp.max(jnp.where(own, off, -1), axis=1, keepdims=True)
        want = jnp.where(rank == 0, lo, jnp.where(hi == lo, NEVER, hi))
        value = jnp.sum(
            jnp.where(own & (off == want), jnp.broadcast_to(gate_x, off.shape), 0.0),
            axis=1,
            keepdims=True,
        )
        gates[0, x * devices * MOST : (x + 1) * devices * MOST, :] = jnp.broadcast_to(
            value, (devices * MOST, gates.shape[2])
        )

    def slot(ref, index):
        return ref.at[pl.ds(pl.multiple_of(index * block, block), block), :]

    def go_copy(d):
        to = lax.rem(me + d, devices)
        return pltpu.make_async_remote_copy(
            src_ref=slot(out_rows, to // ctx_count),
            dst_ref=slot(in_rows, me),
            send_sem=go_send.at[d],
            recv_sem=go_recv.at[d],
            device_id=(to // ctx_count, lax.rem(to, ctx_count)),
            device_id_type=MESH,
        )

    def back_copy(d):
        to = lax.rem(me + d, devices)
        return pltpu.make_async_remote_copy(
            src_ref=slot(reply_rows, to),
            dst_ref=slot(back_rows, me),
            send_sem=back_send.at[d],
            recv_sem=back_recv.at[d],
            device_id=(to // ctx_count, lax.rem(to, ctx_count)),
            device_id_type=MESH,
        )

    def arrived(ref, sems, d):
        source = lax.rem(me + devices - d, devices)
        pltpu.make_async_remote_copy(
            src_ref=slot(ref, source),
            dst_ref=slot(ref, source),
            send_sem=sems.at[d],
            recv_sem=sems.at[d],
            device_id=(source // ctx_count, lax.rem(source, ctx_count)),
            device_id_type=MESH,
        ).wait_recv()

    def gate_copy(d):
        return pltpu.make_async_remote_copy(
            src_ref=gates.at[0],
            dst_ref=gates.at[d],
            send_sem=gate_send.at[d],
            recv_sem=gate_recv.at[d],
            device_id=(e, lax.rem(c + d, ctx_count)),
            device_id_type=MESH,
        )

    depth = exp_count // 4
    z, y, k = e // 4, lax.rem(e // 2, 2), lax.rem(e, 2)

    def member(z_at, y_at, k_at):
        return z_at * 4 + y_at * 2 + k_at

    def weight_copy(o, to, send, recv):
        return pltpu.make_async_remote_copy(
            src_ref=rows_of(o),
            dst_ref=rows_of(o),
            send_sem=send,
            recv_sem=recv,
            device_id=(to, c),
            device_id_type=MESH,
        )

    y_peer = member(z, 1 - y, k)
    k_peer = member(z, y, 1 - k)

    def up_copy(t):
        return weight_copy(member(z - t + 1, y, k), member(z + 1, y, k), z_send.at[0, t], z_recv.at[0, t])

    def down_copy(t):
        return weight_copy(member(z + t - 1, y, k), member(z - 1, y, k), z_send.at[1, t], z_recv.at[1, t])

    def goes_up(t):
        return (z + 1 < depth) & (z - t + 1 >= 0)

    def goes_down(t):
        return (z >= 1) & (z + t - 1 < depth)

    def y_copy(at):
        return weight_copy(member(at, y, k), y_peer, y_send.at[at], y_recv.at[at])

    def y_in(at):
        return weight_copy(member(at, 1 - y, k), y_peer, y_send.at[at], y_recv.at[at])

    def k_copy(at, across):
        y_at = 1 - y if across else y
        n = at + depth * across
        return weight_copy(member(at, y_at, k), k_peer, c_send.at[n], c_recv.at[n])

    def k_in(at, across):
        y_at = 1 - y if across else y
        n = at + depth * across
        return weight_copy(member(at, y_at, 1 - k), k_peer, c_send.at[n], c_recv.at[n])

    def send_along(t):
        @pl.when(goes_up(t))
        def _():
            up_copy(t).start()

        @pl.when(goes_down(t))
        def _():
            down_copy(t).start()

    def hop(t):
        if t >= depth:
            return

        @pl.when(z - t >= 0)
        def _():
            weight_copy(member(z - t, y, k), k_peer, z_send.at[0, t], z_recv.at[0, t]).wait_recv()
            if t + 1 < depth:

                @pl.when(goes_up(t + 1))
                def _():
                    up_copy(t + 1).start()

            y_copy(z - t).start()
            k_copy(z - t, 0).start()

        @pl.when(z + t < depth)
        def _():
            weight_copy(member(z + t, y, k), k_peer, z_send.at[1, t], z_recv.at[1, t]).wait_recv()
            if t + 1 < depth:

                @pl.when(goes_down(t + 1))
                def _():
                    down_copy(t + 1).start()

            y_copy(z + t).start()
            k_copy(z + t, 0).start()

    def relay_y(i):
        at = lax.rem(z + i, depth)
        y_in(at).wait_recv()
        k_copy(at, 1).start()

    pl.semaphore_wait(barrier, devices - 1)

    def start_go(d, carry):
        go_copy(d).start()
        return carry

    lax.fori_loop(1, devices, start_go, 0)
    for d in range(1, ctx_count):
        gate_copy(d).start()
    for copy in own_cols:
        copy.wait()
    send_along(1)
    y_copy(z).start()
    k_copy(z, 0).start()

    in_rows[pl.ds(pl.multiple_of(me * block, block), block), :] = out_rows[
        pl.ds(pl.multiple_of(e * block, block), block), :
    ]
    m = iota((padded, in_count), 1)
    n = iota((padded, in_count), 0)
    per = devices * MOST
    matches = (
        (m // block == lax.rem(n, per) // MOST)
        & (lax.rem(m, group) // MOST == n // per)
        & (lax.rem(m, MOST) == lax.rem(n, MOST))
    )
    unfold = [
        onehot(matches & (lax.rem(m, block) // group == f)) for f in range(FOLD)
    ]

    def wait_go(d, carry):
        arrived(in_rows, go_recv, d)
        return carry

    lax.fori_loop(1, devices, wait_go, 0)
    received = in_rows[...]
    tokens = jnp.concatenate(
        [dot(u, received).astype(jnp.bfloat16) for u in unfold], axis=1
    )
    for d in range(1, ctx_count):
        gate_copy(d).wait_recv()
    parts = []
    for x in range(local_experts):
        chosen = tokens[x * per : (x + 1) * per, :]
        loads[3 * x].wait()
        gate_part = dot(chosen, wg[x])
        loads[3 * x + 1].wait()
        up_part = dot(chosen, wu[x])
        hidden = (gate_part / (1.0 + jnp.exp(-gate_part)) * up_part).astype(jnp.bfloat16)
        loads[3 * x + 2].wait()
        expert_out = dot(hidden, wd[x])
        factor = gates[0, x * per : (x + 1) * per, 0:1]
        for d in range(1, ctx_count):
            factor = factor + gates[d, x * per : (x + 1) * per, 0:1]
        parts.append((expert_out * factor).astype(jnp.bfloat16))
        if x == 0:
            hop(1)
            relay_y(0)
    weighted = jnp.concatenate(parts, axis=0)
    m = iota((in_count, padded), 0)
    n = iota((in_count, padded), 1)
    back = onehot(
        (m // block == lax.rem(n, per) // MOST)
        & (lax.rem(m, group) // MOST == n // per)
        & (lax.rem(m, MOST) == lax.rem(n, MOST))
    )
    part = lax.rem(iota((in_count, 1), 0), block) // group
    folded = jnp.zeros((in_count, fold), jnp.float32)
    for f in range(FOLD):
        folded = jnp.where(part == f, dot(back, weighted[:, f * fold : (f + 1) * fold]), folded)
    reply_rows[...] = folded.astype(jnp.bfloat16)

    def start_back(d, carry):
        back_copy(d).start()
        return carry

    lax.fori_loop(1, devices, start_back, 0)
    back_rows[pl.ds(pl.multiple_of(me * block, block), block), :] = reply_rows[
        pl.ds(pl.multiple_of(me * block, block), block), :
    ]
    for t in range(2, min(3, depth)):
        hop(t)

    def wait_back(d, carry):
        arrived(back_rows, back_recv, d)
        return carry

    lax.fori_loop(1, devices, wait_back, 0)
    returned = back_rows[...]
    along = lax.rem(iota((rows, in_count), 1), block) // group
    moe = []
    for f in range(FOLD):
        hits = jnp.where(along == f, spread[...], jnp.zeros_like(spread[...]))
        moe.append(dot(hits, returned))
    layer = (x_ref[...].astype(jnp.float32) + jnp.concatenate(moe, axis=1)).astype(jnp.bfloat16)
    layer_ref[...] = layer
    widened = layer.astype(jnp.float32)
    scale = lax.rsqrt(jnp.mean(widened * widened, axis=1, keepdims=True) + EPSILON)

    def table_rows(index):
        return pl.ds(pl.multiple_of(index * rows, rows), rows)

    table[table_rows(c), :] = (widened * scale * gain_ref[...]).astype(jnp.bfloat16)

    def row_copy(d, owner):
        return pltpu.make_async_remote_copy(
            src_ref=table.at[table_rows(owner), :],
            dst_ref=table.at[table_rows(owner), :],
            send_sem=row_send.at[d],
            recv_sem=row_recv.at[d],
            device_id=(e, lax.rem(c + d, ctx_count)),
            device_id_type=MESH,
        )

    for d in range(1, ctx_count):
        row_copy(d, c).start()
    for t in range(3, depth):
        hop(t)
    for i in range(1, depth):
        relay_y(i)
    for d in range(depth):
        k_in(d, 0).wait_recv()
        k_in(d, 1).wait_recv()

    def project(owner):
        normed = table[table_rows(owner), :]
        for n in range(3):
            cols = slice(n * head_cols, (n + 1) * head_cols)
            proj[table_rows(owner), cols] = dot(normed, weights[:, cols]).astype(jnp.bfloat16)

    project(c)
    for d in range(1, ctx_count):
        owner = lax.rem(c + ctx_count - d, ctx_count)
        row_copy(d, owner).wait_recv()
        project(owner)

    total = table.shape[0]
    allowed = iota((total, total), 1) < count_ref[0]
    per_step = 128 // HEAD_DIM
    steps = head_cols // 128

    def out_copy(d, step):
        to = lax.rem(c + d, ctx_count)
        return pltpu.make_async_remote_copy(
            src_ref=away.at[table_rows(to), step * 128 : (step + 1) * 128],
            dst_ref=context_ref.at[
                :, pl.ds(pl.multiple_of(c * head_cols + step * 128, 128), 128)
            ],
            send_sem=out_send.at[d, step],
            recv_sem=out_recv.at[d, step],
            device_id=(e, to),
            device_id_type=MESH,
        )

    def out_in(d, step):
        source = lax.rem(c + ctx_count - d, ctx_count)
        cols = pl.ds(pl.multiple_of(source * head_cols + step * 128, 128), 128)
        return pltpu.make_async_remote_copy(
            src_ref=context_ref.at[:, cols],
            dst_ref=context_ref.at[:, cols],
            send_sem=out_send.at[d, step],
            recv_sem=out_recv.at[d, step],
            device_id=(e, source),
            device_id_type=MESH,
        )

    for step in range(steps):
        blended = []
        for h in range(step * per_step, (step + 1) * per_step):
            at = h * HEAD_DIM
            query = proj[:, at : at + HEAD_DIM]
            key = proj[:, head_cols + at : head_cols + at + HEAD_DIM]
            value = proj[:, 2 * head_cols + at : 2 * head_cols + at + HEAD_DIM]
            scores = dot_t(query, key, ((1,), (1,))) * (HEAD_DIM ** (-0.5))
            scores = jnp.where(allowed, scores, MASKED)
            top = jnp.max(scores, axis=1, keepdims=True)
            raw = jnp.where(allowed, jnp.exp(scores - top), 0.0)
            denominator = jnp.sum(raw, axis=1, keepdims=True)
            blended.append(dot(raw.astype(jnp.bfloat16), value) / denominator)
        away[:, step * 128 : (step + 1) * 128] = jnp.concatenate(blended, axis=1).astype(
            jnp.bfloat16
        )
        for d in range(1, ctx_count):
            out_copy(d, step).start()
        context_ref[:, pl.ds(pl.multiple_of(c * head_cols + step * 128, 128), 128)] = away[
            table_rows(c), step * 128 : (step + 1) * 128
        ]

    def wait_sends(d, carry):
        go_copy(d).wait_send()
        back_copy(d).wait_send()
        return carry

    lax.fori_loop(1, devices, wait_sends, 0)
    for t in range(1, depth):

        @pl.when(goes_up(t))
        def _():
            up_copy(t).wait_send()

        @pl.when(goes_down(t))
        def _():
            down_copy(t).wait_send()

    for d in range(depth):
        y_copy(d).wait_send()
        k_copy(d, 0).wait_send()
        k_copy(d, 1).wait_send()
    for d in range(1, ctx_count):
        gate_copy(d).wait_send()
        row_copy(d, c).wait_send()
        for step in range(steps):
            out_copy(d, step).wait_send()
            out_in(d, step).wait_recv()


def emit(layer_ref, context_ref, layer_out, context_out, sem):
    copies = [
        pltpu.make_async_copy(layer_ref, layer_out, sem.at[0]),
        pltpu.make_async_copy(context_ref, context_out, sem.at[1]),
    ]
    for copy in copies:
        copy.start()
    for copy in copies:
        copy.wait()


def fused_local(*operands):
    inputs, selected, gate_weight, query_weight = (operands[i] for i in (0, 1, 3, 7))
    exp_count = lax.axis_size("exp")
    ctx_count = lax.axis_size("ctx")
    rows, width = inputs.shape
    local_experts, _, hidden = gate_weight.shape
    devices = exp_count * ctx_count
    block = local_experts * MOST * FOLD
    head_cols = width // ctx_count
    depth = exp_count // 4
    padded = local_experts * devices * MOST
    bf16 = jnp.bfloat16
    dma = pltpu.SemaphoreType.DMA
    vmem = pl.BlockSpec(memory_space=pltpu.VMEM)
    hbm = pl.BlockSpec(memory_space=pl.ANY)
    smem = pl.BlockSpec(memory_space=pltpu.SMEM)
    operands = operands[:1] + (operands[1].T,) + operands[2:6] + (operands[6].reshape(1, width),) + operands[7:]
    results = pl.pallas_call(
        functools.partial(fused, exp_count, ctx_count),
        out_shape=(jax.ShapeDtypeStruct((rows, width), bf16),) * 2,
        in_specs=[vmem, vmem, vmem, hbm, hbm, hbm, vmem, hbm, hbm, hbm, smem],
        out_specs=(vmem, vmem),
        scratch_shapes=[
            pltpu.VMEM((local_experts, width, hidden), bf16),
            pltpu.VMEM((local_experts, width, hidden), bf16),
            pltpu.VMEM((local_experts, hidden, width), bf16),
            pltpu.VMEM((width, 3 * head_cols), bf16),
            pltpu.VMEM((exp_count * block, width // FOLD), bf16),
            pltpu.VMEM((devices * block, width // FOLD), bf16),
            pltpu.VMEM((devices * block, width // FOLD), bf16),
            pltpu.VMEM((devices * block, width // FOLD), bf16),
            pltpu.VMEM((ctx_count, padded, 128), jnp.float32),
            pltpu.VMEM((ctx_count * rows, width), bf16),
            pltpu.VMEM((ctx_count * rows, 3 * head_cols), bf16),
            pltpu.VMEM((ctx_count * rows, head_cols), bf16),
            pltpu.VMEM((rows, devices * block), bf16),
            dma((3 * local_experts,)),
            dma((3,)),
            dma((devices,)),
            dma((devices,)),
            dma((devices,)),
            dma((devices,)),
            dma((ctx_count,)),
            dma((ctx_count,)),
            dma((2, depth)),
            dma((2, depth)),
            dma((depth,)),
            dma((depth,)),
            dma((2 * depth,)),
            dma((2 * depth,)),
            dma((ctx_count,)),
            dma((ctx_count,)),
            dma((ctx_count, head_cols // 128)),
            dma((ctx_count, head_cols // 128)),
        ],
        compiler_params=pltpu.CompilerParams(
            collective_id=0, has_side_effects=True, vmem_limit_bytes=VMEM_LIMIT
        ),
    )(*operands)
    return pl.pallas_call(
        emit,
        out_shape=(jax.ShapeDtypeStruct((rows, width), bf16),) * 2,
        in_specs=[vmem, vmem],
        out_specs=(hbm, hbm),
        scratch_shapes=[dma((2,))],
    )(*results)


def choose(*operands):
    inputs, gate_weight = operands[0], operands[3]
    exp_count, ctx_count = lax.axis_size("exp"), lax.axis_size("ctx")
    rows, width = inputs.shape
    local_experts = gate_weight.shape[0]
    devices = exp_count * ctx_count
    folded_rows = devices * local_experts * MOST * FOLD
    table = rows * ctx_count
    need = (
        3 * 2 * gate_weight.size
        + 6 * width * width // ctx_count
        + 8 * folded_rows * width // FOLD
        + 8 * FOLD * folded_rows * (folded_rows // FOLD)
        + 12 * table * table
    )
    ranks = max(2, (2 * operands[1].shape[1] + exp_count - 1) // exp_count)
    if exp_count % 4 == 0 and ranks == MOST and width // ctx_count % 128 == 0 and need < VMEM_LIMIT // 2:
        return fused_local(*operands)
    return local(*operands)


def solution(mesh):
    placed = (
        P(("exp", "ctx"), None),
        P(None, "ctx"),
        P("exp", "ctx"),
        P("exp", None, "ctx"),
        P("exp", None, "ctx"),
        P("exp", "ctx", None),
        P(),
        P("exp", None),
        P("exp", None),
        P("exp", None),
        P("exp"),
    )
    return jax.shard_map(
        choose,
        mesh=mesh,
        in_specs=placed,
        out_specs=(P(("exp", "ctx"), None), P(("exp", "ctx"), None)),
        check_vma=False,
    )
```
